32 devices in a mesh: tm: 16 (over z, y, x), row: 2 (over core).
Axes of the slice: x: 2, y: 2, z: 4, core: 2. Of those that a mesh axis runs over, the one named last changes fastest.
Arguments:
- initial: float32 [1024], replicated, may hold values from -6 to 6
- dynamics: float32 [1024, 1024], replicated, may hold values from -0.009765625 to 0.009765625
- obs_rows: bfloat16 [32768, 1024], P('tm', 'row'), may hold values from -0.1875 to 0.1875
- obs_values: bfloat16 [32768], P('tm'), may hold values from -6 to 6
- obs_slab: int32 [32768, 1], P('tm'), may hold values from 0 to 31; in each aligned block of 2048 rows (0 to 2047, 2048 to 4095, ...) at most 64 rows name the same one
Outputs:
- states: float32 [32, 1024], P('tm', 'row')
The draws below stay inside these ranges and needn't reach their ends.
Inputs may be any that keep to these rules, and one draw needn't show every extreme that they name: `obs_slab`: within the rows ingested by one index of tm, no slab is named by more than 64 rows, a bound that some block reaches of them.
All inputs are finite; a program needn't handle non-finite values.
Results may differ from the reference program's by a relative error of at most 0.0003.
Values may be sent and summed in bfloat16 or wider, within the bound.
A program may use at most 128 MiB of HBM per device.

```python
import math
import jax
import jax.numpy as jnp
import numpy as np
from jax import lax

S = 1024
OBS_DEV = 2048
CAP = 64
SLABS = 32
OBS = 32768


def block_scale(key, extent, pieces, least, high):
    factor_of = 1.0
    for axis_at, blocks in pieces:
        heights = jax.random.uniform(jax.random.fold_in(jax.random.fold_in(key, 6), axis_at), (blocks,), jnp.float32, least / len(pieces), high / len(pieces))
        factor_of = factor_of * jnp.repeat(jnp.exp(heights), extent[axis_at] // blocks).reshape((-1,) + (1,) * (len(extent) - 1 - axis_at))
    return factor_of


def shared_out(rng, own, number, rows, count, top, reach, lean):
    ranking = jax.random.permutation(rng, count)
    crowded, usual = load_shares(count, rows * top, reach, lean, True), load_shares(count, rows * top, reach, lean, False)
    places = jnp.arange(count)

    def named(lengths, offset_by):
        used = int((lengths > 0).sum())
        fixed = max(1, used // 4)
        passed = fixed + (places - fixed + offset_by * (used - fixed)) % max(1, count - fixed)
        return jnp.zeros((count,), jnp.int32).at[ranking[jnp.where(places < fixed, places, passed)]].set(jnp.asarray(lengths, jnp.int32))

    lengths = jnp.where(number % 4 == 0, named(crowded, number // 4), named(usual, number - number // 4 - 1))
    mixed = jax.random.permutation(jax.random.fold_in(own, 3), count)
    giver, sink = mixed[0:count // 2 * 2:2], mixed[1:count // 2 * 2:2]
    margin = jnp.minimum(lengths[giver] - 1, reach - lengths[sink]) // 2
    margin = jnp.where((giver == ranking[0]) | (sink == ranking[0]) | (lengths[sink] == 0), 0, jnp.maximum(margin, 0))
    passed = jax.random.randint(jax.random.fold_in(own, 4), (count // 2,), 0, 1 << 20) % (margin + 1)
    lengths = lengths.at[giver].add(-passed).at[sink].add(passed)
    members = jnp.searchsorted(jnp.cumsum(lengths), jnp.arange(rows * top), side="right").astype(jnp.int32)
    grid = members.reshape(top, rows).T
    grid = grid[jax.random.permutation(jax.random.fold_in(own, 1), rows)]
    offset_by = jax.random.randint(jax.random.fold_in(own, 2), (rows, 1), 0, top)
    return jnp.take_along_axis(grid, (jnp.arange(top)[None, :] + offset_by) % top, axis=1)


def load_shares(amount, total, reach, lean, full):
    portions = [(1 << 20) // math.isqrt(rank ** lean) + 1 for rank in range(1, amount + 1)]
    largest = reach if full else min(reach, max(-(-total // amount), total * portions[0] // sum(portions)))
    least = 1 if total - largest >= amount - 1 else 0
    given, spare = [largest] + [least] * (amount - 1), total - largest - least * (amount - 1)
    while spare > 0:
        free = [i for i in range(1, amount) if given[i] < largest] or [i for i in range(1, amount) if given[i] < reach]
        pool, budget = sum([portions[i] for i in free]), spare
        for i in free:
            extra = min(reach - given[i], max(1, budget * portions[i] // pool), spare)
            given[i] = given[i] + extra
            spare = spare - extra
    return np.array(given)


def centred(own_key, shape, deviation, bound, pieces=(), held_as=jnp.bfloat16):
    array = jax.random.normal(own_key, shape, jnp.float32) * deviation
    if len(pieces) > 0:
        array = block_scale(own_key, shape, pieces, -0.22, 0.18) * array
    return jnp.clip(array, min=-bound, max=bound).astype(held_as)


def setup_inputs(seed: int = 0) -> dict:
    streams_of = jax.random.split(jax.random.key(seed), 6)
    initial = centred(streams_of[0], (S,), 1.0, 6.0, (), jnp.float32)
    dynamics = centred(streams_of[1], (S, S), (400 * S) ** -0.5, 0.009765625, (), jnp.float32)
    obs_rows = centred(streams_of[2], (OBS, S), S ** -0.5, 0.1875, ((0, 16), (1, 2)))
    obs_values = centred(streams_of[3], (OBS,), 1.0, 6.0, ((0, 16),))
    obs_slab_keys = jax.random.split(jax.random.fold_in(streams_of[4], 1), OBS // OBS_DEV)
    obs_slab_turns = jax.random.permutation(jax.random.fold_in(streams_of[4], 3), OBS // OBS_DEV)
    obs_slab = jax.vmap(lambda own, number: shared_out(jax.random.fold_in(streams_of[4], 2), own, number, OBS_DEV, SLABS, 1, CAP, 2))(obs_slab_keys, obs_slab_turns).reshape((OBS, 1))
    return dict(initial=initial, dynamics=dynamics, obs_rows=obs_rows, obs_values=obs_values, obs_slab=obs_slab)


def reference(initial, dynamics, obs_rows, obs_values, obs_slab):
    evolve = jnp.eye(S, dtype=jnp.float32) + dynamics
    rows_f32 = obs_rows.astype(jnp.float32)
    values_f32 = obs_values.astype(jnp.float32)
    target = obs_slab[:, 0]

    def advance(state, slab_index):
        moved = jnp.dot(evolve, state, precision=lax.Precision.HIGHEST)
        in_slab = (target == slab_index).astype(jnp.float32)
        misfit = in_slab * (values_f32 - jnp.dot(rows_f32, moved, precision=lax.Precision.HIGHEST))
        updated = moved + 0.3 * jnp.dot(misfit, rows_f32, precision=lax.Precision.HIGHEST)
        return updated, updated

    final_state, states = lax.scan(advance, initial, jnp.arange(SLABS, dtype=jnp.int32))
    return states
```

```python
import functools

import jax
import jax.numpy as jnp
from jax import lax
from jax.experimental import pallas as pl
from jax.experimental.pallas import tpu as pltpu
from jax.sharding import PartitionSpec as P

CAP = 64
LANES = 128
MESH = pl.DeviceIdType.MESH

sigma_gain = 0.3


def sort_kernel(slabs, target_ref, rows_ref, values_ref, sent_ref, sent_values_ref, slot_ref):
    count = target_ref.shape[1]
    block = 256
    before = (
        lax.broadcasted_iota(jnp.int32, (block, block), 0)
        < lax.broadcasted_iota(jnp.int32, (block, block), 1)
    ).astype(jnp.float32).astype(jnp.bfloat16)
    slab_of = lax.broadcasted_iota(jnp.int32, (slabs, block), 0)
    carry = (slab_of[:, :1] * CAP).astype(jnp.float32)
    for start in range(0, count, block):
        named = (target_ref[:, start : start + block] == slab_of).astype(jnp.float32)
        ahead = jnp.dot(named.astype(jnp.bfloat16), before, preferred_element_type=jnp.float32)
        slot = jnp.sum(named * (ahead + carry), axis=0, keepdims=True)
        slot_ref[:, start : start + block] = slot.astype(jnp.int32)
        carry = carry + jnp.sum(named, axis=1, keepdims=True)

    values = jnp.broadcast_to(values_ref[...].astype(jnp.float32), (8, count)).astype(jnp.bfloat16)

    def place(step, _):
        first = pl.multiple_of(step * block, block)
        wanted = lax.broadcasted_iota(jnp.int32, (block, count), 0) + first
        pick = (wanted == slot_ref[...]).astype(jnp.float32).astype(jnp.bfloat16)
        sent_ref[pl.ds(first, block), :] = jnp.dot(
            pick, rows_ref[...], preferred_element_type=jnp.float32
        ).astype(jnp.bfloat16)
        sent_values_ref[:, pl.ds(first, block)] = lax.dot_general(
            values, pick, (((1,), (1,)), ((), ())), preferred_element_type=jnp.float32
        )[:1].astype(jnp.bfloat16)
        return 0

    lax.fori_loop(0, slabs * CAP // block, place, 0)


def sort_rows(obs_rows, obs_values, target, slabs):
    count, cols = obs_rows.shape
    slots = slabs * CAP
    vmem = pl.BlockSpec(memory_space=pltpu.VMEM)
    return pl.pallas_call(
        functools.partial(sort_kernel, slabs),
        out_shape=(
            jax.ShapeDtypeStruct((slots, cols), jnp.bfloat16),
            jax.ShapeDtypeStruct((1, slots), jnp.bfloat16),
        ),
        in_specs=[vmem] * 3,
        out_specs=(vmem, vmem),
        scratch_shapes=[pltpu.VMEM((1, count), jnp.int32)],
        compiler_params=pltpu.CompilerParams(vmem_limit_bytes=48 << 20),
        name="sort_rows",
    )(target, obs_rows, obs_values)


def chain_kernel(
    devices, a_ref, b_ref, start_ref, out_ref, perm, came, went, back, barred, send_sem, recv_sem
):
    t, r = lax.axis_index("tm"), lax.axis_index("row")
    place = 2 * t + r
    after = (t + r, 1 - r)
    ahead = (t + r - 1, 1 - r)
    subs = came.shape[0]
    state = subs * LANES

    barrier = pltpu.get_barrier_semaphore()

    @pl.when(place > 0)
    def _():
        pl.semaphore_signal(barrier, inc=1, device_id=ahead, device_id_type=MESH)

    @pl.when(place < devices - 1)
    def _():
        pl.semaphore_signal(barrier, inc=1, device_id=after, device_id_type=MESH)

    for sub in range(subs):
        perm[:, sub, :] = a_ref[sub * LANES : (sub + 1) * LANES, :]

    at_end = (place == 0) | (place == devices - 1)

    @pl.when(at_end)
    def _():
        pl.semaphore_wait(barrier, 1)

    @pl.when(jnp.logical_not(at_end))
    def _():
        pl.semaphore_wait(barrier, 2)

    onward = pltpu.make_async_remote_copy(
        src_ref=went, dst_ref=came, send_sem=send_sem.at[0], recv_sem=recv_sem.at[0],
        device_id=after, device_id_type=MESH,
    )
    answer = pltpu.make_async_remote_copy(
        src_ref=went, dst_ref=back, send_sem=send_sem.at[1], recv_sem=recv_sem.at[1],
        device_id=ahead, device_id_type=MESH,
    )

    @pl.when(place == 0)
    def _():
        came[...] = start_ref[...]

    @pl.when(place > 0)
    def _():
        onward.wait_recv()

    entering = came[...]
    pieces = [jnp.broadcast_to(entering[k : k + 1, :], (subs, LANES)) for k in range(subs)]
    lane = lax.broadcasted_iota(jnp.int32, (subs, LANES), 1)
    group = 16

    def rows(step, total):
        for inner in range(group):
            g = step * group + inner
            part = perm[g, :, 0:LANES] * pieces[0]
            for k in range(1, subs):
                part = part + perm[g, :, k * LANES : (k + 1) * LANES] * pieces[k]
            total = jnp.where(lane == g, jnp.sum(part, axis=1, keepdims=True), total)
        return total

    leaving = lax.fori_loop(0, LANES // group, rows, jnp.zeros((subs, LANES), jnp.float32))
    leaving = leaving + b_ref[...]
    went[...] = leaving

    @pl.when(place < devices - 1)
    def _():
        onward.start()

    half = subs // 2

    @pl.when(r == 1)
    def _():
        answer.start()
        out_ref[0] = came[half:, :]
        out_ref[1] = went[half:, :]
        answer.wait_send()

    @pl.when(r == 0)
    def _():
        answer.wait_recv()
        out_ref[0] = went[:half, :]
        out_ref[1] = back[:half, :]

    @pl.when(place < devices - 1)
    def _():
        onward.wait_send()


def run_chain(transition, offset, initial, devices):
    width = transition.shape[0]
    subs = width // LANES
    vmem = pl.BlockSpec(memory_space=pltpu.VMEM)
    small = pltpu.VMEM((subs, LANES), jnp.float32)
    states = pl.pallas_call(
        functools.partial(chain_kernel, devices),
        out_shape=jax.ShapeDtypeStruct((2, subs // 2, LANES), jnp.float32),
        in_specs=[vmem] * 3,
        out_specs=vmem,
        scratch_shapes=[
            pltpu.VMEM((LANES, subs, width), jnp.float32),
            small,
            small,
            small,
            small,
            pltpu.SemaphoreType.DMA((2,)),
            pltpu.SemaphoreType.DMA((2,)),
        ],
        compiler_params=pltpu.CompilerParams(
            collective_id=0, has_side_effects=True, vmem_limit_bytes=48 << 20
        ),
        name="chain",
    )(transition, offset.reshape(subs, LANES), initial.reshape(subs, LANES))
    return states.reshape(2, width // 2)


def split(value):
    high = lax.reduce_precision(value, 8, 7)
    low = lax.reduce_precision(value - high, 8, 7)
    return high.astype(jnp.bfloat16), low.astype(jnp.bfloat16)


def dot32(left, right, dims):
    return lax.dot_general(left, right, (dims, ((), ())), preferred_element_type=jnp.float32)


def body(initial, dynamics, obs_rows, obs_values, obs_slab):
    time_devs = lax.axis_size("tm")
    row_devs = lax.axis_size("row")
    width = dynamics.shape[1]
    cols = obs_rows.shape[1]
    slabs = time_devs * row_devs
    sent, sent_values = sort_rows(
        obs_rows, obs_values.reshape(1, -1), obs_slab.reshape(1, -1), slabs
    )
    axes = ("tm", "row")
    got = lax.all_to_all(
        sent.reshape(slabs, CAP, cols), axes, split_axis=0, concat_axis=0, tiled=True
    )
    got_values = lax.all_to_all(
        sent_values.reshape(slabs, CAP), axes, split_axis=0, concat_axis=0, tiled=True
    )
    got = got.reshape(time_devs, row_devs, CAP, cols)
    values = got_values.reshape(time_devs, row_devs, CAP)[:, 0].reshape(1, -1)
    rows = got.transpose(0, 2, 1, 3).reshape(time_devs * CAP, width)
    high, low = split(dynamics)
    seen = rows.astype(jnp.float32) + (
        dot32(rows, high, ((1,), (0,))) + dot32(rows, low, ((1,), (0,)))
    )
    seen_high, seen_low = split(seen)
    gain = dot32(rows, seen_high, ((0,), (0,))) + dot32(rows, seen_low, ((0,), (0,)))
    transition = jnp.eye(width, dtype=jnp.float32) + dynamics - sigma_gain * gain
    offset = sigma_gain * dot32(values, rows, ((1,), (0,)))
    return run_chain(transition, offset, initial, slabs)


def solution(mesh):
    placed = (P(), P(), P("tm", "row"), P("tm"), P("tm", None))
    return jax.shard_map(
        body, mesh=mesh, in_specs=placed, out_specs=P("tm", "row"), check_vma=False
    )
```

```python
import jax
import jax.numpy as jnp
from jax import lax
from jax.experimental import pallas as pl
from jax.experimental.pallas import tpu as pltpu
from jax.sharding import PartitionSpec as P

CAP = 64
LANES = 128
MESH = pl.DeviceIdType.MESH

sigma_gain = 0.3


def route_kernel(
    target_ref, rows_ref, values_ref, got_ref, got_values_ref,
    sent, sent_values, slot_ref, row_send, row_recv, value_send, value_recv, own_sem,
):
    time_devs, row_devs = lax.axis_size("tm"), lax.axis_size("row")
    slabs = time_devs * row_devs
    me = lax.axis_index("tm") * row_devs + lax.axis_index("row")
    count = target_ref.shape[1]
    block = 256
    share = block // CAP
    blocks = slabs // share

    def device(slab):
        return (slab // row_devs, lax.rem(slab, row_devs))

    barrier = pltpu.get_barrier_semaphore()

    def greet(slab, _):
        @pl.when(slab != me)
        def _():
            pl.semaphore_signal(barrier, inc=1, device_id=device(slab), device_id_type=MESH)

        return 0

    lax.fori_loop(0, slabs, greet, 0)

    before = (
        lax.broadcasted_iota(jnp.int32, (block, block), 0)
        < lax.broadcasted_iota(jnp.int32, (block, block), 1)
    ).astype(jnp.float32).astype(jnp.bfloat16)
    slab_of = lax.broadcasted_iota(jnp.int32, (slabs, block), 0)
    carry = (slab_of[:, :1] * CAP).astype(jnp.float32)
    for start in range(0, count, block):
        named = (target_ref[:, start : start + block] == slab_of).astype(jnp.float32)
        ahead = jnp.dot(named.astype(jnp.bfloat16), before, preferred_element_type=jnp.float32)
        slot = jnp.sum(named * (ahead + carry), axis=0, keepdims=True)
        slot_ref[:, start : start + block] = slot.astype(jnp.int32)
        carry = carry + jnp.sum(named, axis=1, keepdims=True)

    values = jnp.broadcast_to(values_ref[...].astype(jnp.float32), (8, count)).astype(jnp.bfloat16)
    sent_values[...] = jnp.zeros_like(sent_values)

    def copies(slab, source):
        rows = pltpu.make_async_remote_copy(
            src_ref=sent.at[slab], dst_ref=got_ref.at[source],
            send_sem=row_send.at[slab], recv_sem=row_recv.at[source],
            device_id=device(slab), device_id_type=MESH,
        )
        tags = pltpu.make_async_remote_copy(
            src_ref=sent_values.at[slab], dst_ref=got_values_ref.at[source],
            send_sem=value_send.at[slab], recv_sem=value_recv.at[source],
            device_id=device(slab), device_id_type=MESH,
        )
        return rows, tags

    keep = (
        pltpu.make_async_copy(sent.at[me], got_ref.at[me], own_sem.at[0]),
        pltpu.make_async_copy(sent_values.at[me], got_values_ref.at[me], own_sem.at[1]),
    )

    def place(at):
        first = at * share
        wanted = lax.broadcasted_iota(jnp.int32, (block, count), 0) + first * CAP
        pick = (wanted == slot_ref[...]).astype(jnp.float32).astype(jnp.bfloat16)
        rows = jnp.dot(pick, rows_ref[...], preferred_element_type=jnp.float32).astype(jnp.bfloat16)
        tags = lax.dot_general(
            values, pick, (((1,), (1,)), ((), ())), preferred_element_type=jnp.float32
        )[:1]
        for inner in range(share):
            sent[first + inner] = rows[inner * CAP : (inner + 1) * CAP]
            sent_values[first + inner, :, :CAP] = tags[:, inner * CAP : (inner + 1) * CAP]

    def send(at):
        for inner in range(share):
            slab = at * share + inner

            @pl.when(slab != me)
            def _():
                for copy in copies(slab, me):
                    copy.start()

            @pl.when(slab == me)
            def _():
                for copy in keep:
                    copy.start()

    mine = me // share
    place(mine)
    pl.semaphore_wait(barrier, slabs - 1)
    send(mine)

    def step(turn, _):
        at = lax.rem(mine + turn, blocks)
        place(at)
        send(at)
        return 0

    lax.fori_loop(1, blocks, step, 0)

    def finish(slab, _):
        @pl.when(slab != me)
        def _():
            for copy in copies(slab, slab):
                copy.wait_recv()
                copy.wait_send()

        return 0

    lax.fori_loop(0, slabs, finish, 0)
    for copy in keep:
        copy.wait()


def route(obs_rows, obs_values, target, slabs):
    count, cols = obs_rows.shape
    vmem = pl.BlockSpec(memory_space=pltpu.VMEM)
    sems = pltpu.SemaphoreType.DMA((slabs,))
    return pl.pallas_call(
        route_kernel,
        out_shape=(
            jax.ShapeDtypeStruct((slabs, CAP, cols), jnp.bfloat16),
            jax.ShapeDtypeStruct((slabs, 1, LANES), jnp.float32),
        ),
        in_specs=[vmem] * 3,
        out_specs=(vmem, vmem),
        scratch_shapes=[
            pltpu.VMEM((slabs, CAP, cols), jnp.bfloat16),
            pltpu.VMEM((slabs, 1, LANES), jnp.float32),
            pltpu.VMEM((1, count), jnp.int32),
            sems,
            sems,
            sems,
            sems,
            pltpu.SemaphoreType.DMA((2,)),
        ],
        compiler_params=pltpu.CompilerParams(
            collective_id=1, has_side_effects=True, vmem_limit_bytes=56 << 20
        ),
        name="route",
    )(target, obs_rows, obs_values)


def chain_kernel(
    high_ref, low_ref, b_ref, start_ref, out_ref,
    perm, high_got, low_got, b_got, came, went, back, offset, send_sem, recv_sem, tile_send, tile_recv,
):
    t, r = lax.axis_index("tm"), lax.axis_index("row")
    last = lax.axis_size("tm") - 1
    partner = (t, 1 - r)
    subs = came.shape[0]
    width = subs * LANES
    tile = 256
    tiles = width // tile

    barrier = pltpu.get_barrier_semaphore()

    def greet(peer):
        pl.semaphore_signal(barrier, inc=1, device_id=peer, device_id_type=MESH)

    greet(partner)

    @pl.when(t > 0)
    def _():
        greet((t - 1, 1))

    @pl.when((r == 1) & (t < last))
    def _():
        greet((t + 1, 0))
        greet((t + 1, 1))

    peers = 1 + jnp.where(t > 0, 1, 0) + jnp.where((r == 1) & (t < last), 2, 0)
    pl.semaphore_wait(barrier, peers)

    def push(source, target, index, peer):
        return pltpu.make_async_remote_copy(
            src_ref=source, dst_ref=target, send_sem=send_sem.at[index],
            recv_sem=recv_sem.at[index], device_id=peer, device_id_type=MESH,
        )

    lend = push(b_ref, b_got, 0, partner)
    answer = push(went, back, 1, partner)
    onward = push(went, came, 2, (t + 1, 1))
    aside = pltpu.make_async_remote_copy(
        src_ref=went, dst_ref=came, send_sem=send_sem.at[3],
        recv_sem=recv_sem.at[2], device_id=(t + 1, 0), device_id_type=MESH,
    )

    def part(k):
        cols = pl.ds(pl.multiple_of(k * tile, tile), tile)
        return [
            pltpu.make_async_remote_copy(
                src_ref=source.at[:, cols], dst_ref=target.at[:, cols],
                send_sem=tile_send.at[index, k], recv_sem=tile_recv.at[index, k],
                device_id=partner, device_id_type=MESH,
            )
            for index, (source, target) in enumerate(((high_ref, high_got), (low_ref, low_got)))
        ]

    @pl.when(r == 0)
    def _():
        lend.start()
        for k in range(tiles):
            for copy in part(k):
                copy.start()

    for sub in range(subs):
        own = slice(sub * LANES, (sub + 1) * LANES)
        perm[:, sub, :] = high_ref[own, :].astype(jnp.float32) + low_ref[own, :].astype(jnp.float32)

    lane = lax.broadcasted_iota(jnp.int32, (subs, LANES), 1)
    group = 16

    def apply(vector):
        pieces = [jnp.broadcast_to(vector[k : k + 1, :], (subs, LANES)) for k in range(subs)]

        def rows(step, total):
            for inner in range(group):
                g = step * group + inner
                part = perm[g, :, 0:LANES] * pieces[0]
                for k in range(1, subs):
                    part = part + perm[g, :, k * LANES : (k + 1) * LANES] * pieces[k]
                total = jnp.where(lane == g, jnp.sum(part, axis=1, keepdims=True), total)
            return total

        return lax.fori_loop(0, LANES // group, rows, jnp.zeros((subs, LANES), jnp.float32))

    offset[...] = b_ref[...]

    @pl.when(r == 1)
    def _():
        lend.wait_recv()
        offset[...] = apply(b_got[...]) + b_ref[...]

        def compose(k, _):
            for copy in part(k):
                copy.wait_recv()
            cols = pl.ds(pl.multiple_of(k * tile, tile), tile)
            high, low = high_got[:, cols], low_got[:, cols]
            whole = (
                jnp.dot(high_ref[...], high, preferred_element_type=jnp.float32)
                + jnp.dot(high_ref[...], low, preferred_element_type=jnp.float32)
                + jnp.dot(low_ref[...], high, preferred_element_type=jnp.float32)
            )
            for sub in range(subs):
                perm[:, sub, cols] = whole[sub * LANES : (sub + 1) * LANES, :]
            return 0

        lax.fori_loop(0, tiles, compose, 0)

    @pl.when(r == 0)
    def _():
        lend.wait_send()

        def drain(k, _):
            for copy in part(k):
                copy.wait_send()
            return 0

        lax.fori_loop(0, tiles, drain, 0)

    @pl.when(t == 0)
    def _():
        came[...] = start_ref[...]

    @pl.when(t > 0)
    def _():
        onward.wait_recv()

    went[...] = apply(came[...]) + offset[...]
    passing = (r == 1) & (t < last)

    @pl.when(passing)
    def _():
        onward.start()
        aside.start()

    answer.start()
    answer.wait()
    half = subs // 2

    @pl.when(r == 0)
    def _():
        out_ref[0] = went[:half, :]
        out_ref[1] = back[:half, :]

    @pl.when(r == 1)
    def _():
        out_ref[0] = back[half:, :]
        out_ref[1] = went[half:, :]

    @pl.when(passing)
    def _():
        onward.wait_send()
        aside.wait_send()


def run_chain(high, low, offset, initial):
    width = high.shape[0]
    subs = width // LANES
    tiles = width // 256
    vmem = pl.BlockSpec(memory_space=pltpu.VMEM)
    small = pltpu.VMEM((subs, LANES), jnp.float32)
    states = pl.pallas_call(
        chain_kernel,
        out_shape=jax.ShapeDtypeStruct((2, subs // 2, LANES), jnp.float32),
        in_specs=[vmem] * 4,
        out_specs=vmem,
        scratch_shapes=[
            pltpu.VMEM((LANES, subs, width), jnp.float32),
            pltpu.VMEM((width, width), jnp.bfloat16),
            pltpu.VMEM((width, width), jnp.bfloat16),
            small,
            small,
            small,
            small,
            small,
            pltpu.SemaphoreType.DMA((4,)),
            pltpu.SemaphoreType.DMA((3,)),
            pltpu.SemaphoreType.DMA((2, tiles)),
            pltpu.SemaphoreType.DMA((2, tiles)),
        ],
        compiler_params=pltpu.CompilerParams(
            collective_id=0, has_side_effects=True, vmem_limit_bytes=48 << 20
        ),
        name="chain",
    )(high, low, offset.reshape(subs, LANES), initial.reshape(subs, LANES))
    return states.reshape(2, width // 2)


def split(value):
    high = lax.reduce_precision(value, 8, 7)
    low = lax.reduce_precision(value - high, 8, 7)
    return high.astype(jnp.bfloat16), low.astype(jnp.bfloat16)


def dot32(left, right, dims):
    return lax.dot_general(left, right, (dims, ((), ())), preferred_element_type=jnp.float32)


def body(initial, dynamics, obs_rows, obs_values, obs_slab):
    time_devs = lax.axis_size("tm")
    row_devs = lax.axis_size("row")
    width = dynamics.shape[1]
    cols = obs_rows.shape[1]
    slabs = time_devs * row_devs
    got, got_values = route(obs_rows, obs_values.reshape(1, -1), obs_slab.reshape(1, -1), slabs)
    got = got.reshape(time_devs, row_devs, CAP, cols)
    values = got_values[:, 0, :CAP].astype(jnp.bfloat16).reshape(time_devs, row_devs, CAP)[:, 0].reshape(1, -1)
    rows = got.transpose(0, 2, 1, 3).reshape(time_devs * CAP, width)
    high, low = split(dynamics)
    seen = rows.astype(jnp.float32) + (
        dot32(rows, high, ((1,), (0,))) + dot32(rows, low, ((1,), (0,)))
    )
    seen_high, seen_low = split(seen)
    gain = dot32(rows, seen_high, ((0,), (0,))) + dot32(rows, seen_low, ((0,), (0,)))
    transition = jnp.eye(width, dtype=jnp.float32) + dynamics - sigma_gain * gain
    offset = sigma_gain * dot32(values, rows, ((1,), (0,)))
    return run_chain(*split(transition), offset, initial)


def solution(mesh):
    placed = (P(), P(), P("tm", "row"), P("tm"), P("tm", None))
    return jax.shard_map(
        body, mesh=mesh, in_specs=placed, out_specs=P("tm", "row"), check_vma=False
    )
```

```python
import jax
import jax.numpy as jnp
from jax import lax
from jax.experimental import pallas as pl
from jax.experimental.pallas import tpu as pltpu
from jax.sharding import PartitionSpec as P

CAP = 64
LANES = 128
MESH = pl.DeviceIdType.MESH

sigma_gain = 0.3


def observer_kernel(
    target_ref, rows_ref, values_ref, dynamics_ref, start_ref, out_ref,
    sent, sent_values, slot_ref, got, got_values, dynamics, dyn_high, dyn_low, turned, gain, moment,
    high_ref, low_ref, b_ref, perm, high_got, low_got, b_got, came, went, back, offset,
    row_send, row_recv, value_send, value_recv, own_sem, send_sem, recv_sem, tile_send, tile_recv,
):
    time_devs, row_devs = lax.axis_size("tm"), lax.axis_size("row")
    t, r = lax.axis_index("tm"), lax.axis_index("row")
    slabs = time_devs * row_devs
    last = time_devs - 1
    me = t * row_devs + r
    partner = (t, 1 - r)
    count, local = rows_ref.shape
    width = local * row_devs
    subs = width // LANES
    tile = 256
    tiles = width // tile
    block = 256
    share = block // CAP
    blocks = slabs // share

    def device(slab):
        return (slab // row_devs, lax.rem(slab, row_devs))

    barrier = pltpu.get_barrier_semaphore()

    def greet(slab, _):
        @pl.when(slab != me)
        def _():
            pl.semaphore_signal(barrier, inc=1, device_id=device(slab), device_id_type=MESH)

        return 0

    lax.fori_loop(0, slabs, greet, 0)
    fetch = pltpu.make_async_copy(dynamics_ref, dynamics, own_sem.at[2])
    fetch.start()

    before = (
        lax.broadcasted_iota(jnp.int32, (block, block), 0)
        < lax.broadcasted_iota(jnp.int32, (block, block), 1)
    ).astype(jnp.float32).astype(jnp.bfloat16)
    slab_of = lax.broadcasted_iota(jnp.int32, (slabs, block), 0)
    carry = (slab_of[:, :1] * CAP).astype(jnp.float32)
    for start in range(0, count, block):
        named = (target_ref[:, start : start + block] == slab_of).astype(jnp.float32)
        ahead = jnp.dot(named.astype(jnp.bfloat16), before, preferred_element_type=jnp.float32)
        slot = jnp.sum(named * (ahead + carry), axis=0, keepdims=True)
        slot_ref[:, start : start + block] = slot.astype(jnp.int32)
        carry = carry + jnp.sum(named, axis=1, keepdims=True)

    values = jnp.broadcast_to(values_ref[...].astype(jnp.float32), (8, count)).astype(jnp.bfloat16)
    sent_values[...] = jnp.zeros_like(sent_values)

    def landing(source):
        rows = pl.ds(pl.multiple_of(source // row_devs * CAP, CAP), CAP)
        cols = pl.ds(pl.multiple_of(lax.rem(source, row_devs) * local, local), local)
        return got.at[rows, cols]

    def copies(slab, source):
        rows = pltpu.make_async_remote_copy(
            src_ref=sent.at[slab], dst_ref=landing(source),
            send_sem=row_send.at[slab], recv_sem=row_recv.at[source],
            device_id=device(slab), device_id_type=MESH,
        )
        tags = pltpu.make_async_remote_copy(
            src_ref=sent_values.at[slab], dst_ref=got_values.at[source],
            send_sem=value_send.at[slab], recv_sem=value_recv.at[source],
            device_id=device(slab), device_id_type=MESH,
        )
        return rows, tags

    keep = (
        pltpu.make_async_copy(sent.at[me], landing(me), own_sem.at[0]),
        pltpu.make_async_copy(sent_values.at[me], got_values.at[me], own_sem.at[1]),
    )

    def place(at):
        first = at * share
        wanted = lax.broadcasted_iota(jnp.int32, (block, count), 0) + first * CAP
        pick = (wanted == slot_ref[...]).astype(jnp.float32).astype(jnp.bfloat16)
        rows = jnp.dot(pick, rows_ref[...], preferred_element_type=jnp.float32).astype(jnp.bfloat16)
        tags = lax.dot_general(
            values, pick, (((1,), (1,)), ((), ())), preferred_element_type=jnp.float32
        )[:1]
        for inner in range(share):
            sent[first + inner] = rows[inner * CAP : (inner + 1) * CAP]
            sent_values[first + inner, :, :CAP] = tags[:, inner * CAP : (inner + 1) * CAP]

    def send(at):
        for inner in range(share):
            slab = at * share + inner

            @pl.when(slab != me)
            def _():
                for copy in copies(slab, me):
                    copy.start()

            @pl.when(slab == me)
            def _():
                for copy in keep:
                    copy.start()

    mine = me // share
    place(mine)
    pl.semaphore_wait(barrier, slabs - 1)
    send(mine)

    def step(turn, _):
        at = lax.rem(mine + turn, blocks)
        place(at)
        send(at)
        return 0

    lax.fori_loop(1, blocks, step, 0)

    fetch.wait()

    def divide(k, _):
        rows = pl.ds(pl.multiple_of(k * LANES, LANES), LANES)
        high = dynamics[rows, :].astype(jnp.bfloat16)
        dyn_high[rows, :] = high
        dyn_low[rows, :] = (dynamics[rows, :] - high.astype(jnp.float32)).astype(jnp.bfloat16)
        return 0

    lax.fori_loop(0, subs, divide, 0)
    gain[...] = jnp.zeros_like(gain)
    moment[...] = jnp.zeros_like(moment)

    chips = block // CAP
    groups = time_devs // chips
    nearest = t // chips

    def gather(turn, _):
        at = jnp.where(nearest * 2 < groups, nearest + turn, nearest + groups - turn)
        at = lax.rem(at, groups)

        def arrive(source, _):
            @pl.when(source != me)
            def _():
                for copy in copies(source, source):
                    copy.wait_recv()

            @pl.when(source == me)
            def _():
                for copy in keep:
                    copy.wait()

            return 0

        lax.fori_loop(at * chips * row_devs, (at + 1) * chips * row_devs, arrive, 0)
        own = pl.ds(pl.multiple_of(at * block, block), block)
        rows = got[own, :]
        turned[...] = rows.T
        tags = jnp.concatenate(
            [got_values[(at * chips + k) * row_devs][:, :CAP] for k in range(chips)], axis=1
        )
        tags = jnp.broadcast_to(tags, (8, block)).astype(jnp.bfloat16)
        moment[...] += jnp.dot(tags, rows, preferred_element_type=jnp.float32)

        def column(k, _):
            cols = pl.ds(pl.multiple_of(k * tile, tile), tile)
            seen = (
                got[own, cols].astype(jnp.float32)
                + jnp.dot(got[own, :], dyn_high[:, cols], preferred_element_type=jnp.float32)
                + jnp.dot(got[own, :], dyn_low[:, cols], preferred_element_type=jnp.float32)
            )
            high = seen.astype(jnp.bfloat16)
            low = (seen - high.astype(jnp.float32)).astype(jnp.bfloat16)
            gain[:, cols] += jnp.dot(
                turned[...], high, preferred_element_type=jnp.float32
            ) + jnp.dot(turned[...], low, preferred_element_type=jnp.float32)
            return 0

        lax.fori_loop(0, tiles, column, 0)
        return 0

    lax.fori_loop(0, groups, gather, 0)

    def push(source, target, index, peer):
        return pltpu.make_async_remote_copy(
            src_ref=source, dst_ref=target, send_sem=send_sem.at[index],
            recv_sem=recv_sem.at[index], device_id=peer, device_id_type=MESH,
        )

    lend = push(b_ref, b_got, 0, partner)
    answer = push(went, back, 1, partner)
    onward = push(went, came, 2, (t + 1, 1))
    aside = pltpu.make_async_remote_copy(
        src_ref=went, dst_ref=came, send_sem=send_sem.at[3],
        recv_sem=recv_sem.at[2], device_id=(t + 1, 0), device_id_type=MESH,
    )

    def part(k):
        cols = pl.ds(pl.multiple_of(k * tile, tile), tile)
        return [
            pltpu.make_async_remote_copy(
                src_ref=source.at[:, cols], dst_ref=target.at[:, cols],
                send_sem=tile_send.at[index, k], recv_sem=tile_recv.at[index, k],
                device_id=partner, device_id_type=MESH,
            )
            for index, (source, target) in enumerate(((high_ref, high_got), (low_ref, low_got)))
        ]

    for sub in range(subs):
        b_ref[sub : sub + 1, :] = sigma_gain * moment[:1, sub * LANES : (sub + 1) * LANES]

    @pl.when(r == 0)
    def _():
        lend.start()

    def settle(k, _):
        cols = pl.ds(pl.multiple_of(k * tile, tile), tile)
        for sub in range(subs):
            own = slice(sub * LANES, (sub + 1) * LANES)
            diagonal = (
                lax.broadcasted_iota(jnp.int32, (LANES, tile), 0) + sub * LANES
                == lax.broadcasted_iota(jnp.int32, (LANES, tile), 1) + k * tile
            ).astype(jnp.float32)
            whole = diagonal + dynamics[own, cols] - sigma_gain * gain[own, cols]
            high = whole.astype(jnp.bfloat16)
            high_ref[own, cols] = high
            low_ref[own, cols] = (whole - high.astype(jnp.float32)).astype(jnp.bfloat16)
            perm[:, sub, cols] = whole

        @pl.when(r == 0)
        def _():
            for copy in part(k):
                copy.start()

        return 0

    lax.fori_loop(0, tiles, settle, 0)

    lane = lax.broadcasted_iota(jnp.int32, (subs, LANES), 1)
    group = 16

    def apply(vector):
        pieces = [jnp.broadcast_to(vector[k : k + 1, :], (subs, LANES)) for k in range(subs)]

        def rows(step, total):
            for inner in range(group):
                g = step * group + inner
                part = perm[g, :, 0:LANES] * pieces[0]
                for k in range(1, subs):
                    part = part + perm[g, :, k * LANES : (k + 1) * LANES] * pieces[k]
                total = jnp.where(lane == g, jnp.sum(part, axis=1, keepdims=True), total)
            return total

        return lax.fori_loop(0, LANES // group, rows, jnp.zeros((subs, LANES), jnp.float32))

    offset[...] = b_ref[...]

    @pl.when(r == 1)
    def _():
        lend.wait_recv()
        offset[...] = apply(b_got[...]) + b_ref[...]

        def compose(k, _):
            for copy in part(k):
                copy.wait_recv()
            cols = pl.ds(pl.multiple_of(k * tile, tile), tile)
            high, low = high_got[:, cols], low_got[:, cols]
            whole = (
                jnp.dot(high_ref[...], high, preferred_element_type=jnp.float32)
                + jnp.dot(high_ref[...], low, preferred_element_type=jnp.float32)
                + jnp.dot(low_ref[...], high, preferred_element_type=jnp.float32)
            )
            for sub in range(subs):
                perm[:, sub, cols] = whole[sub * LANES : (sub + 1) * LANES, :]
            return 0

        lax.fori_loop(0, tiles, compose, 0)

    @pl.when(r == 0)
    def _():
        lend.wait_send()

        def drain(k, _):
            for copy in part(k):
                copy.wait_send()
            return 0

        lax.fori_loop(0, tiles, drain, 0)

    @pl.when(t == 0)
    def _():
        came[...] = start_ref[...]

    @pl.when(t > 0)
    def _():
        onward.wait_recv()

    went[...] = apply(came[...]) + offset[...]
    passing = (r == 1) & (t < last)

    @pl.when(passing)
    def _():
        onward.start()
        aside.start()

    answer.start()
    answer.wait()
    half = subs // 2

    @pl.when(r == 0)
    def _():
        out_ref[0] = went[:half, :]
        out_ref[1] = back[:half, :]

    @pl.when(r == 1)
    def _():
        out_ref[0] = back[half:, :]
        out_ref[1] = went[half:, :]

    @pl.when(passing)
    def _():
        onward.wait_send()
        aside.wait_send()

    def finish(slab, _):
        @pl.when(slab != me)
        def _():
            for copy in copies(slab, slab):
                copy.wait_send()

        return 0

    lax.fori_loop(0, slabs, finish, 0)


def body(initial, dynamics, obs_rows, obs_values, obs_slab):
    time_devs = lax.axis_size("tm")
    row_devs = lax.axis_size("row")
    width = dynamics.shape[1]
    count, local = obs_rows.shape
    slabs = time_devs * row_devs
    subs = width // LANES
    tiles = width // 256
    vmem = pl.BlockSpec(memory_space=pltpu.VMEM)
    small = pltpu.VMEM((subs, LANES), jnp.float32)
    square = pltpu.VMEM((width, width), jnp.bfloat16)
    square32 = pltpu.VMEM((width, width), jnp.float32)
    sems = pltpu.SemaphoreType.DMA((slabs,))
    states = pl.pallas_call(
        observer_kernel,
        out_shape=jax.ShapeDtypeStruct((2, subs // 2, LANES), jnp.float32),
        in_specs=[vmem, vmem, vmem, pl.BlockSpec(memory_space=pl.ANY), vmem],
        out_specs=vmem,
        scratch_shapes=[
            pltpu.VMEM((slabs, CAP, local), jnp.bfloat16),
            pltpu.VMEM((slabs, 1, LANES), jnp.float32),
            pltpu.VMEM((1, count), jnp.int32),
            pltpu.VMEM((time_devs * CAP, width), jnp.bfloat16),
            pltpu.VMEM((slabs, 1, LANES), jnp.float32),
            square32,
            square,
            square,
            pltpu.VMEM((width, 256), jnp.bfloat16),
            square32,
            pltpu.VMEM((8, width), jnp.float32),
            square,
            square,
            small,
            pltpu.VMEM((LANES, subs, width), jnp.float32),
            square,
            square,
            small,
            small,
            small,
            small,
            small,
            sems,
            sems,
            sems,
            sems,
            pltpu.SemaphoreType.DMA((3,)),
            pltpu.SemaphoreType.DMA((4,)),
            pltpu.SemaphoreType.DMA((3,)),
            pltpu.SemaphoreType.DMA((2, tiles)),
            pltpu.SemaphoreType.DMA((2, tiles)),
        ],
        compiler_params=pltpu.CompilerParams(
            collective_id=0, has_side_effects=True, vmem_limit_bytes=60 << 20
        ),
        name="observer",
    )(
        obs_slab.reshape(1, -1),
        obs_rows,
        obs_values.reshape(1, -1),
        dynamics,
        initial.reshape(subs, LANES),
    )
    return states.reshape(2, width // 2)


def solution(mesh):
    placed = (P(), P(), P("tm", "row"), P("tm"), P("tm", None))
    return jax.shard_map(
        body, mesh=mesh, in_specs=placed, out_specs=P("tm", "row"), check_vma=False
    )
```

```python
import jax
import jax.numpy as jnp
from jax import lax
from jax.experimental import pallas as pl
from jax.experimental.pallas import tpu as pltpu
from jax.sharding import PartitionSpec as P

CAP = 64
LANES = 128
MESH = pl.DeviceIdType.MESH

sigma_gain = 0.3


def chip_at(place):
    turn = place & 3
    turn = jnp.where((place >> 2) & 1 == 1, 3 - turn, turn)
    return (place - (place & 3)) + jnp.where(turn < 2, turn, 5 - turn)


def place_of(chip):
    turn = chip & 3
    turn = jnp.where(turn < 2, turn, 5 - turn)
    return (chip - (chip & 3)) + jnp.where((chip >> 2) & 1 == 1, 3 - turn, turn)


def observer_kernel(
    target_ref, rows_ref, values_ref, dynamics_ref, start_ref, out_ref,
    sent, sent_values, slot_ref, got, got_values, dynamics, dyn_high, dyn_low, turned, gain, moment,
    high_ref, low_ref, b_ref, perm, high_got, low_got, b_got, came, went, back, offset, owner_ref,
    row_send, row_recv, value_send, value_recv, own_sem, send_sem, recv_sem, tile_send, tile_recv, out_send, out_recv,
):
    time_devs, row_devs = lax.axis_size("tm"), lax.axis_size("row")
    t, r = lax.axis_index("tm"), lax.axis_index("row")
    slabs = time_devs * row_devs
    last = time_devs - 1
    place_here = place_of(t)
    after = chip_at(jnp.minimum(place_here + 1, last))
    me = t * row_devs + r
    partner = (t, 1 - r)
    count, local = rows_ref.shape
    width = local * row_devs
    subs = width // LANES
    tile = 256
    tiles = width // tile
    block = 256
    share = block // CAP
    blocks = slabs // share

    def device(slab):
        return (slab // row_devs, lax.rem(slab, row_devs))

    barrier = pltpu.get_barrier_semaphore()

    def greet(slab, _):
        @pl.when(slab != me)
        def _():
            pl.semaphore_signal(barrier, inc=1, device_id=device(slab), device_id_type=MESH)

        return 0

    lax.fori_loop(0, slabs, greet, 0)
    fetch = pltpu.make_async_copy(dynamics_ref, dynamics, own_sem.at[2])
    fetch.start()

    before = (
        lax.broadcasted_iota(jnp.int32, (block, block), 0)
        < lax.broadcasted_iota(jnp.int32, (block, block), 1)
    ).astype(jnp.float32).astype(jnp.bfloat16)
    slab_of = lax.broadcasted_iota(jnp.int32, (slabs, block), 0)
    carry = (slab_of[:, :1] * CAP).astype(jnp.float32)
    pair = row_devs.bit_length() - 1
    target = target_ref[...]
    owner_ref[...] = (chip_at(target >> pair) << pair) + (target & (row_devs - 1))
    for start in range(0, count, block):
        named = (owner_ref[:, start : start + block] == slab_of).astype(jnp.float32)
        ahead = jnp.dot(named.astype(jnp.bfloat16), before, preferred_element_type=jnp.float32)
        slot = jnp.sum(named * (ahead + carry), axis=0, keepdims=True)
        slot_ref[:, start : start + block] = slot.astype(jnp.int32)
        carry = carry + jnp.sum(named, axis=1, keepdims=True)

    values = jnp.broadcast_to(values_ref[...].astype(jnp.float32), (8, count)).astype(jnp.bfloat16)
    sent_values[...] = jnp.zeros_like(sent_values)

    def landing(source):
        rows = pl.ds(pl.multiple_of(source // row_devs * CAP, CAP), CAP)
        cols = pl.ds(pl.multiple_of(lax.rem(source, row_devs) * local, local), local)
        return got.at[rows, cols]

    def copies(slab, source):
        rows = pltpu.make_async_remote_copy(
            src_ref=sent.at[slab], dst_ref=landing(source),
            send_sem=row_send.at[slab], recv_sem=row_recv.at[source],
            device_id=device(slab), device_id_type=MESH,
        )
        tags = pltpu.make_async_remote_copy(
            src_ref=sent_values.at[slab], dst_ref=got_values.at[source],
            send_sem=value_send.at[slab], recv_sem=value_recv.at[source],
            device_id=device(slab), device_id_type=MESH,
        )
        return rows, tags

    keep = (
        pltpu.make_async_copy(sent.at[me], landing(me), own_sem.at[0]),
        pltpu.make_async_copy(sent_values.at[me], got_values.at[me], own_sem.at[1]),
    )

    def place(at):
        first = at * share
        wanted = lax.broadcasted_iota(jnp.int32, (block, count), 0) + first * CAP
        pick = (wanted == slot_ref[...]).astype(jnp.float32).astype(jnp.bfloat16)
        rows = jnp.dot(pick, rows_ref[...], preferred_element_type=jnp.float32).astype(jnp.bfloat16)
        tags = lax.dot_general(
            values, pick, (((1,), (1,)), ((), ())), preferred_element_type=jnp.float32
        )[:1]
        for inner in range(share):
            sent[first + inner] = rows[inner * CAP : (inner + 1) * CAP]
            sent_values[first + inner, :, :CAP] = tags[:, inner * CAP : (inner + 1) * CAP]

    def send(at):
        for inner in range(share):
            slab = at * share + inner

            @pl.when(slab != me)
            def _():
                for copy in copies(slab, me):
                    copy.start()

            @pl.when(slab == me)
            def _():
                for copy in keep:
                    copy.start()

    mine = me // share
    place(mine)
    pl.semaphore_wait(barrier, slabs - 1)
    send(mine)

    def step(turn, _):
        at = lax.rem(mine + turn, blocks)
        place(at)
        send(at)
        return 0

    lax.fori_loop(1, blocks, step, 0)

    fetch.wait()

    def divide(k, _):
        rows = pl.ds(pl.multiple_of(k * LANES, LANES), LANES)
        high = dynamics[rows, :].astype(jnp.bfloat16)
        dyn_high[rows, :] = high
        dyn_low[rows, :] = (dynamics[rows, :] - high.astype(jnp.float32)).astype(jnp.bfloat16)
        return 0

    lax.fori_loop(0, subs, divide, 0)
    gain[...] = jnp.zeros_like(gain)
    moment[...] = jnp.zeros_like(moment)

    chips = block // CAP
    groups = time_devs // chips
    nearest = t // chips

    def gather(turn, _):
        at = jnp.where(nearest * 2 < groups, nearest + turn, nearest + groups - turn)
        at = lax.rem(at, groups)

        def arrive(source, _):
            @pl.when(source != me)
            def _():
                for copy in copies(source, source):
                    copy.wait_recv()

            @pl.when(source == me)
            def _():
                for copy in keep:
                    copy.wait()

            return 0

        lax.fori_loop(at * chips * row_devs, (at + 1) * chips * row_devs, arrive, 0)
        own = pl.ds(pl.multiple_of(at * block, block), block)
        rows = got[own, :]
        turned[...] = rows.T
        tags = jnp.concatenate(
            [got_values[(at * chips + k) * row_devs][:, :CAP] for k in range(chips)], axis=1
        )
        tags = jnp.broadcast_to(tags, (8, block)).astype(jnp.bfloat16)
        moment[...] += jnp.dot(tags, rows, preferred_element_type=jnp.float32)

        def column(k, _):
            cols = pl.ds(pl.multiple_of(k * tile, tile), tile)
            seen = (
                got[own, cols].astype(jnp.float32)
                + jnp.dot(got[own, :], dyn_high[:, cols], preferred_element_type=jnp.float32)
                + jnp.dot(got[own, :], dyn_low[:, cols], preferred_element_type=jnp.float32)
            )
            high = seen.astype(jnp.bfloat16)
            low = (seen - high.astype(jnp.float32)).astype(jnp.bfloat16)
            gain[:, cols] += jnp.dot(
                turned[...], high, preferred_element_type=jnp.float32
            ) + jnp.dot(turned[...], low, preferred_element_type=jnp.float32)
            return 0

        lax.fori_loop(0, tiles, column, 0)
        return 0

    lax.fori_loop(0, groups, gather, 0)

    def push(source, target, index, peer):
        return pltpu.make_async_remote_copy(
            src_ref=source, dst_ref=target, send_sem=send_sem.at[index],
            recv_sem=recv_sem.at[index], device_id=peer, device_id_type=MESH,
        )

    lend = push(b_ref, b_got, 0, partner)
    onward = push(went, came, 2, (after, 1))
    aside = pltpu.make_async_remote_copy(
        src_ref=went, dst_ref=came, send_sem=send_sem.at[3],
        recv_sem=recv_sem.at[2], device_id=(after, 0), device_id_type=MESH,
    )

    def part(k):
        cols = pl.ds(pl.multiple_of(k * tile, tile), tile)
        return [
            pltpu.make_async_remote_copy(
                src_ref=source.at[:, cols], dst_ref=target.at[:, cols],
                send_sem=tile_send.at[index, k], recv_sem=tile_recv.at[index, k],
                device_id=partner, device_id_type=MESH,
            )
            for index, (source, target) in enumerate(((high_ref, high_got), (low_ref, low_got)))
        ]

    for sub in range(subs):
        b_ref[sub : sub + 1, :] = sigma_gain * moment[:1, sub * LANES : (sub + 1) * LANES]

    @pl.when(r == 0)
    def _():
        lend.start()

    def settle(k, _):
        cols = pl.ds(pl.multiple_of(k * tile, tile), tile)
        for sub in range(subs):
            own = slice(sub * LANES, (sub + 1) * LANES)
            diagonal = (
                lax.broadcasted_iota(jnp.int32, (LANES, tile), 0) + sub * LANES
                == lax.broadcasted_iota(jnp.int32, (LANES, tile), 1) + k * tile
            ).astype(jnp.float32)
            whole = diagonal + dynamics[own, cols] - sigma_gain * gain[own, cols]
            high = whole.astype(jnp.bfloat16)
            high_ref[own, cols] = high
            low_ref[own, cols] = (whole - high.astype(jnp.float32)).astype(jnp.bfloat16)
            perm[:, sub, cols] = whole

        @pl.when(r == 0)
        def _():
            for copy in part(k):
                copy.start()

        return 0

    lax.fori_loop(0, tiles, settle, 0)

    lane = lax.broadcasted_iota(jnp.int32, (subs, LANES), 1)
    group = 16

    def apply(vector):
        pieces = [jnp.broadcast_to(vector[k : k + 1, :], (subs, LANES)) for k in range(subs)]

        def rows(step, total):
            for inner in range(group):
                g = step * group + inner
                part = perm[g, :, 0:LANES] * pieces[0]
                for k in range(1, subs):
                    part = part + perm[g, :, k * LANES : (k + 1) * LANES] * pieces[k]
                total = jnp.where(lane == g, jnp.sum(part, axis=1, keepdims=True), total)
            return total

        return lax.fori_loop(0, LANES // group, rows, jnp.zeros((subs, LANES), jnp.float32))

    offset[...] = b_ref[...]

    @pl.when(r == 1)
    def _():
        lend.wait_recv()
        offset[...] = apply(b_got[...]) + b_ref[...]

        def compose(k, _):
            for copy in part(k):
                copy.wait_recv()
            cols = pl.ds(pl.multiple_of(k * tile, tile), tile)
            high, low = high_got[:, cols], low_got[:, cols]
            whole = (
                jnp.dot(high_ref[...], high, preferred_element_type=jnp.float32)
                + jnp.dot(high_ref[...], low, preferred_element_type=jnp.float32)
                + jnp.dot(low_ref[...], high, preferred_element_type=jnp.float32)
            )
            for sub in range(subs):
                perm[:, sub, cols] = whole[sub * LANES : (sub + 1) * LANES, :]
            return 0

        lax.fori_loop(0, tiles, compose, 0)

    @pl.when(r == 0)
    def _():
        lend.wait_send()

        def drain(k, _):
            for copy in part(k):
                copy.wait_send()
            return 0

        lax.fori_loop(0, tiles, drain, 0)

    @pl.when(place_here == 0)
    def _():
        came[...] = start_ref[...]

    @pl.when(place_here > 0)
    def _():
        onward.wait_recv()

    went[...] = apply(came[...]) + offset[...]
    passing = (r == 1) & (place_here < last)

    @pl.when(passing)
    def _():
        onward.start()
        aside.start()

    stays = place_here == t

    def report(core, sender):
        return pltpu.make_async_remote_copy(
            src_ref=went, dst_ref=back.at[sender], send_sem=out_send.at[core],
            recv_sem=out_recv.at[sender], device_id=(place_here, core), device_id_type=MESH,
        )

    for core in range(2):
        @pl.when(jnp.logical_not(stays & (r == core)))
        def _():
            report(core, r).start()

        @pl.when(stays & (r == core))
        def _():
            back[core] = went[...]

    for core in range(2):
        @pl.when(jnp.logical_not(stays & (r == core)))
        def _():
            report(core, core).wait_recv()
            report(core, r).wait_send()

    half = subs // 2

    @pl.when(r == 0)
    def _():
        out_ref[0] = back[0, :half, :]
        out_ref[1] = back[1, :half, :]

    @pl.when(r == 1)
    def _():
        out_ref[0] = back[0, half:, :]
        out_ref[1] = back[1, half:, :]

    @pl.when(passing)
    def _():
        onward.wait_send()
        aside.wait_send()

    def finish(slab, _):
        @pl.when(slab != me)
        def _():
            for copy in copies(slab, slab):
                copy.wait_send()

        return 0

    lax.fori_loop(0, slabs, finish, 0)


def body(initial, dynamics, obs_rows, obs_values, obs_slab):
    time_devs = lax.axis_size("tm")
    row_devs = lax.axis_size("row")
    width = dynamics.shape[1]
    count, local = obs_rows.shape
    slabs = time_devs * row_devs
    subs = width // LANES
    tiles = width // 256
    vmem = pl.BlockSpec(memory_space=pltpu.VMEM)
    small = pltpu.VMEM((subs, LANES), jnp.float32)
    square = pltpu.VMEM((width, width), jnp.bfloat16)
    square32 = pltpu.VMEM((width, width), jnp.float32)
    sems = pltpu.SemaphoreType.DMA((slabs,))
    states = pl.pallas_call(
        observer_kernel,
        out_shape=jax.ShapeDtypeStruct((2, subs // 2, LANES), jnp.float32),
        in_specs=[vmem, vmem, vmem, pl.BlockSpec(memory_space=pl.ANY), vmem],
        out_specs=vmem,
        scratch_shapes=[
            pltpu.VMEM((slabs, CAP, local), jnp.bfloat16),
            pltpu.VMEM((slabs, 1, LANES), jnp.float32),
            pltpu.VMEM((1, count), jnp.int32),
            pltpu.VMEM((time_devs * CAP, width), jnp.bfloat16),
            pltpu.VMEM((slabs, 1, LANES), jnp.float32),
            square32,
            square,
            square,
            pltpu.VMEM((width, 256), jnp.bfloat16),
            square32,
            pltpu.VMEM((8, width), jnp.float32),
            square,
            square,
            small,
            pltpu.VMEM((LANES, subs, width), jnp.float32),
            square,
            square,
            small,
            small,
            small,
            pltpu.VMEM((2, subs, LANES), jnp.float32),
            small,
            pltpu.VMEM((1, count), jnp.int32),
            sems,
            sems,
            sems,
            sems,
            pltpu.SemaphoreType.DMA((3,)),
            pltpu.SemaphoreType.DMA((4,)),
            pltpu.SemaphoreType.DMA((3,)),
            pltpu.SemaphoreType.DMA((2, tiles)),
            pltpu.SemaphoreType.DMA((2, tiles)),
            pltpu.SemaphoreType.DMA((2,)),
            pltpu.SemaphoreType.DMA((2,)),
        ],
        compiler_params=pltpu.CompilerParams(
            collective_id=0, has_side_effects=True, vmem_limit_bytes=60 << 20
        ),
        name="observer",
    )(
        obs_slab.reshape(1, -1),
        obs_rows,
        obs_values.reshape(1, -1),
        dynamics,
        initial.reshape(subs, LANES),
    )
    return states.reshape(2, width // 2)


def solution(mesh):
    placed = (P(), P(), P("tm", "row"), P("tm"), P("tm", None))
    return jax.shard_map(
        body, mesh=mesh, in_specs=placed, out_specs=P("tm", "row"), check_vma=False
    )
```

```python
import jax
import jax.numpy as jnp
from jax import lax
from jax.experimental import pallas as pl
from jax.experimental.pallas import tpu as pltpu
from jax.sharding import PartitionSpec as P

CAP = 64
LANES = 128
MESH = pl.DeviceIdType.MESH

sigma_gain = 0.3


def visit(own, turn, total):
    if total & (total - 1):
        return lax.rem(own + turn, total)
    if total == 4:
        turn = ((turn & 1) << 1) | (turn >> 1)
    return own ^ turn


def chip_at(place):
    turn = place & 3
    turn = jnp.where((place >> 2) & 1 == 1, 3 - turn, turn)
    return (place - (place & 3)) + jnp.where(turn < 2, turn, 5 - turn)


def place_of(chip):
    turn = chip & 3
    turn = jnp.where(turn < 2, turn, 5 - turn)
    return (chip - (chip & 3)) + jnp.where((chip >> 2) & 1 == 1, 3 - turn, turn)


def observer_kernel(
    target_ref, rows_ref, values_ref, dynamics_ref, start_ref, out_ref,
    sent, sent_values, slot_ref, got, got_values, dynamics, dyn_high, dyn_low, turned, gain, moment,
    high_ref, low_ref, b_ref, perm, high_got, low_got, b_got, came, went, back, offset, owner_ref,
    row_send, row_recv, value_send, value_recv, own_sem, send_sem, recv_sem, tile_send, tile_recv, out_send, out_recv,
):
    time_devs, row_devs = lax.axis_size("tm"), lax.axis_size("row")
    t, r = lax.axis_index("tm"), lax.axis_index("row")
    slabs = time_devs * row_devs
    last = time_devs - 1
    place_here = place_of(t)
    after = chip_at(jnp.minimum(place_here + 1, last))
    me = t * row_devs + r
    partner = (t, 1 - r)
    count, local = rows_ref.shape
    width = local * row_devs
    subs = width // LANES
    tile = 256
    tiles = width // tile
    block = 256
    share = block // CAP
    blocks = slabs // share

    def device(slab):
        return (slab // row_devs, lax.rem(slab, row_devs))

    barrier = pltpu.get_barrier_semaphore()

    def greet(slab, _):
        @pl.when(slab != me)
        def _():
            pl.semaphore_signal(barrier, inc=1, device_id=device(slab), device_id_type=MESH)

        return 0

    lax.fori_loop(0, slabs, greet, 0)
    fetch = pltpu.make_async_copy(dynamics_ref, dynamics, own_sem.at[2])
    fetch.start()

    before = (
        lax.broadcasted_iota(jnp.int32, (block, block), 0)
        < lax.broadcasted_iota(jnp.int32, (block, block), 1)
    ).astype(jnp.float32).astype(jnp.bfloat16)
    slab_of = lax.broadcasted_iota(jnp.int32, (slabs, block), 0)
    carry = (slab_of[:, :1] * CAP).astype(jnp.float32)
    pair = row_devs.bit_length() - 1
    target = target_ref[...]
    owner_ref[...] = (chip_at(target >> pair) << pair) + (target & (row_devs - 1))
    for start in range(0, count, block):
        named = (owner_ref[:, start : start + block] == slab_of).astype(jnp.float32)
        ahead = jnp.dot(named.astype(jnp.bfloat16), before, preferred_element_type=jnp.float32)
        slot = jnp.sum(named * (ahead + carry), axis=0, keepdims=True)
        slot_ref[:, start : start + block] = slot.astype(jnp.int32)
        carry = carry + jnp.sum(named, axis=1, keepdims=True)

    values = jnp.broadcast_to(values_ref[...].astype(jnp.float32), (8, count)).astype(jnp.bfloat16)
    sent_values[...] = jnp.zeros_like(sent_values)

    def landing(source):
        rows = pl.ds(pl.multiple_of(source // row_devs * CAP, CAP), CAP)
        cols = pl.ds(pl.multiple_of(lax.rem(source, row_devs) * local, local), local)
        return got.at[rows, cols]

    def copies(slab, source):
        rows = pltpu.make_async_remote_copy(
            src_ref=sent.at[slab], dst_ref=landing(source),
            send_sem=row_send.at[slab], recv_sem=row_recv.at[source],
            device_id=device(slab), device_id_type=MESH,
        )
        tags = pltpu.make_async_remote_copy(
            src_ref=sent_values.at[slab], dst_ref=got_values.at[source],
            send_sem=value_send.at[slab], recv_sem=value_recv.at[source],
            device_id=device(slab), device_id_type=MESH,
        )
        return rows, tags

    keep = (
        pltpu.make_async_copy(sent.at[me], landing(me), own_sem.at[0]),
        pltpu.make_async_copy(sent_values.at[me], got_values.at[me], own_sem.at[1]),
    )

    def place(at):
        first = at * share
        wanted = lax.broadcasted_iota(jnp.int32, (block, count), 0) + first * CAP
        pick = (wanted == slot_ref[...]).astype(jnp.float32).astype(jnp.bfloat16)
        rows = jnp.dot(pick, rows_ref[...], preferred_element_type=jnp.float32).astype(jnp.bfloat16)
        tags = lax.dot_general(
            values, pick, (((1,), (1,)), ((), ())), preferred_element_type=jnp.float32
        )[:1]
        for inner in range(share):
            sent[first + inner] = rows[inner * CAP : (inner + 1) * CAP]
            sent_values[first + inner, :, :CAP] = tags[:, inner * CAP : (inner + 1) * CAP]

    def send(at):
        for inner in range(share):
            slab = at * share + inner

            @pl.when(slab != me)
            def _():
                for copy in copies(slab, me):
                    copy.start()

            @pl.when(slab == me)
            def _():
                for copy in keep:
                    copy.start()

    mine = me // share
    layered = 2
    place(mine)
    pl.semaphore_wait(barrier, slabs - 1)
    send(mine)

    def step(turn, _):
        layer, within = turn // layered, lax.rem(turn, layered)
        at = visit(mine // layered, layer, blocks // layered) * layered
        at = at + lax.rem(mine + within, layered)
        place(at)
        send(at)
        return 0

    lax.fori_loop(1, blocks, step, 0)

    fetch.wait()

    def divide(k, _):
        rows = pl.ds(pl.multiple_of(k * LANES, LANES), LANES)
        high = dynamics[rows, :].astype(jnp.bfloat16)
        dyn_high[rows, :] = high
        dyn_low[rows, :] = (dynamics[rows, :] - high.astype(jnp.float32)).astype(jnp.bfloat16)
        return 0

    lax.fori_loop(0, subs, divide, 0)
    gain[...] = jnp.zeros_like(gain)
    moment[...] = jnp.zeros_like(moment)

    chips = block // CAP
    groups = time_devs // chips
    nearest = t // chips

    def gather(turn, _):
        at = visit(nearest, turn, groups)

        def arrive(source, _):
            @pl.when(source != me)
            def _():
                for copy in copies(source, source):
                    copy.wait_recv()

            @pl.when(source == me)
            def _():
                for copy in keep:
                    copy.wait()

            return 0

        lax.fori_loop(at * chips * row_devs, (at + 1) * chips * row_devs, arrive, 0)
        own = pl.ds(pl.multiple_of(at * block, block), block)
        rows = got[own, :]
        turned[...] = rows.T
        tags = jnp.concatenate(
            [got_values[(at * chips + k) * row_devs][:, :CAP] for k in range(chips)], axis=1
        )
        tags = jnp.broadcast_to(tags, (8, block)).astype(jnp.bfloat16)
        moment[...] += jnp.dot(tags, rows, preferred_element_type=jnp.float32)

        def column(k, _):
            cols = pl.ds(pl.multiple_of(k * tile, tile), tile)
            seen = (
                got[own, cols].astype(jnp.float32)
                + jnp.dot(got[own, :], dyn_high[:, cols], preferred_element_type=jnp.float32)
                + jnp.dot(got[own, :], dyn_low[:, cols], preferred_element_type=jnp.float32)
            )
            high = seen.astype(jnp.bfloat16)
            low = (seen - high.astype(jnp.float32)).astype(jnp.bfloat16)
            gain[:, cols] += jnp.dot(
                turned[...], high, preferred_element_type=jnp.float32
            ) + jnp.dot(turned[...], low, preferred_element_type=jnp.float32)
            return 0

        lax.fori_loop(0, tiles, column, 0)
        return 0

    lax.fori_loop(0, groups, gather, 0)

    def push(source, target, index, peer):
        return pltpu.make_async_remote_copy(
            src_ref=source, dst_ref=target, send_sem=send_sem.at[index],
            recv_sem=recv_sem.at[index], device_id=peer, device_id_type=MESH,
        )

    lend = push(b_ref, b_got, 0, partner)
    onward = push(went, came, 2, (after, 1))
    aside = pltpu.make_async_remote_copy(
        src_ref=went, dst_ref=came, send_sem=send_sem.at[3],
        recv_sem=recv_sem.at[2], device_id=(after, 0), device_id_type=MESH,
    )

    def part(k):
        cols = pl.ds(pl.multiple_of(k * tile, tile), tile)
        return [
            pltpu.make_async_remote_copy(
                src_ref=source.at[:, cols], dst_ref=target.at[:, cols],
                send_sem=tile_send.at[index, k], recv_sem=tile_recv.at[index, k],
                device_id=partner, device_id_type=MESH,
            )
            for index, (source, target) in enumerate(((high_ref, high_got), (low_ref, low_got)))
        ]

    for sub in range(subs):
        b_ref[sub : sub + 1, :] = sigma_gain * moment[:1, sub * LANES : (sub + 1) * LANES]

    @pl.when(r == 0)
    def _():
        lend.start()

    def settle(k, _):
        cols = pl.ds(pl.multiple_of(k * tile, tile), tile)
        for sub in range(subs):
            own = slice(sub * LANES, (sub + 1) * LANES)
            diagonal = (
                lax.broadcasted_iota(jnp.int32, (LANES, tile), 0) + sub * LANES
                == lax.broadcasted_iota(jnp.int32, (LANES, tile), 1) + k * tile
            ).astype(jnp.float32)
            whole = diagonal + dynamics[own, cols] - sigma_gain * gain[own, cols]
            high = whole.astype(jnp.bfloat16)
            high_ref[own, cols] = high
            low_ref[own, cols] = (whole - high.astype(jnp.float32)).astype(jnp.bfloat16)
            perm[:, sub, cols] = whole

        @pl.when(r == 0)
        def _():
            for copy in part(k):
                copy.start()

        return 0

    lax.fori_loop(0, tiles, settle, 0)

    lane = lax.broadcasted_iota(jnp.int32, (subs, LANES), 1)
    group = 16

    def apply(vector):
        pieces = [jnp.broadcast_to(vector[k : k + 1, :], (subs, LANES)) for k in range(subs)]

        def rows(step, total):
            for inner in range(group):
                g = step * group + inner
                part = perm[g, :, 0:LANES] * pieces[0]
                for k in range(1, subs):
                    part = part + perm[g, :, k * LANES : (k + 1) * LANES] * pieces[k]
                total = jnp.where(lane == g, jnp.sum(part, axis=1, keepdims=True), total)
            return total

        return lax.fori_loop(0, LANES // group, rows, jnp.zeros((subs, LANES), jnp.float32))

    offset[...] = b_ref[...]

    @pl.when(r == 1)
    def _():
        lend.wait_recv()
        offset[...] = apply(b_got[...]) + b_ref[...]

        def compose(k, _):
            for copy in part(k):
                copy.wait_recv()
            cols = pl.ds(pl.multiple_of(k * tile, tile), tile)
            high, low = high_got[:, cols], low_got[:, cols]
            whole = (
                jnp.dot(high_ref[...], high, preferred_element_type=jnp.float32)
                + jnp.dot(high_ref[...], low, preferred_element_type=jnp.float32)
                + jnp.dot(low_ref[...], high, preferred_element_type=jnp.float32)
            )
            for sub in range(subs):
                perm[:, sub, cols] = whole[sub * LANES : (sub + 1) * LANES, :]
            return 0

        lax.fori_loop(0, tiles, compose, 0)

    @pl.when(r == 0)
    def _():
        lend.wait_send()

        def drain(k, _):
            for copy in part(k):
                copy.wait_send()
            return 0

        lax.fori_loop(0, tiles, drain, 0)

    @pl.when(place_here == 0)
    def _():
        came[...] = start_ref[...]

    @pl.when(place_here > 0)
    def _():
        onward.wait_recv()

    went[...] = apply(came[...]) + offset[...]
    passing = (r == 1) & (place_here < last)

    @pl.when(passing)
    def _():
        onward.start()
        aside.start()

    stays = place_here == t

    def report(core, sender):
        return pltpu.make_async_remote_copy(
            src_ref=went, dst_ref=back.at[sender], send_sem=out_send.at[core],
            recv_sem=out_recv.at[sender], device_id=(place_here, core), device_id_type=MESH,
        )

    for core in range(2):
        @pl.when(jnp.logical_not(stays & (r == core)))
        def _():
            report(core, r).start()

        @pl.when(stays & (r == core))
        def _():
            back[core] = went[...]

    for core in range(2):
        @pl.when(jnp.logical_not(stays & (r == core)))
        def _():
            report(core, core).wait_recv()
            report(core, r).wait_send()

    half = subs // 2

    @pl.when(r == 0)
    def _():
        out_ref[0] = back[0, :half, :]
        out_ref[1] = back[1, :half, :]

    @pl.when(r == 1)
    def _():
        out_ref[0] = back[0, half:, :]
        out_ref[1] = back[1, half:, :]

    @pl.when(passing)
    def _():
        onward.wait_send()
        aside.wait_send()

    def finish(slab, _):
        @pl.when(slab != me)
        def _():
            for copy in copies(slab, slab):
                copy.wait_send()

        return 0

    lax.fori_loop(0, slabs, finish, 0)


def body(initial, dynamics, obs_rows, obs_values, obs_slab):
    time_devs = lax.axis_size("tm")
    row_devs = lax.axis_size("row")
    width = dynamics.shape[1]
    count, local = obs_rows.shape
    slabs = time_devs * row_devs
    subs = width // LANES
    tiles = width // 256
    vmem = pl.BlockSpec(memory_space=pltpu.VMEM)
    small = pltpu.VMEM((subs, LANES), jnp.float32)
    square = pltpu.VMEM((width, width), jnp.bfloat16)
    square32 = pltpu.VMEM((width, width), jnp.float32)
    sems = pltpu.SemaphoreType.DMA((slabs,))
    states = pl.pallas_call(
        observer_kernel,
        out_shape=jax.ShapeDtypeStruct((2, subs // 2, LANES), jnp.float32),
        in_specs=[vmem, vmem, vmem, pl.BlockSpec(memory_space=pl.ANY), vmem],
        out_specs=vmem,
        scratch_shapes=[
            pltpu.VMEM((slabs, CAP, local), jnp.bfloat16),
            pltpu.VMEM((slabs, 1, LANES), jnp.float32),
            pltpu.VMEM((1, count), jnp.int32),
            pltpu.VMEM((time_devs * CAP, width), jnp.bfloat16),
            pltpu.VMEM((slabs, 1, LANES), jnp.float32),
            square32,
            square,
            square,
            pltpu.VMEM((width, 256), jnp.bfloat16),
            square32,
            pltpu.VMEM((8, width), jnp.float32),
            square,
            square,
            small,
            pltpu.VMEM((LANES, subs, width), jnp.float32),
            square,
            square,
            small,
            small,
            small,
            pltpu.VMEM((2, subs, LANES), jnp.float32),
            small,
            pltpu.VMEM((1, count), jnp.int32),
            sems,
            sems,
            sems,
            sems,
            pltpu.SemaphoreType.DMA((3,)),
            pltpu.SemaphoreType.DMA((4,)),
            pltpu.SemaphoreType.DMA((3,)),
            pltpu.SemaphoreType.DMA((2, tiles)),
            pltpu.SemaphoreType.DMA((2, tiles)),
            pltpu.SemaphoreType.DMA((2,)),
            pltpu.SemaphoreType.DMA((2,)),
        ],
        compiler_params=pltpu.CompilerParams(
            collective_id=0, has_side_effects=True, vmem_limit_bytes=60 << 20
        ),
        name="observer",
    )(
        obs_slab.reshape(1, -1),
        obs_rows,
        obs_values.reshape(1, -1),
        dynamics,
        initial.reshape(subs, LANES),
    )
    return states.reshape(2, width // 2)


def solution(mesh):
    placed = (P(), P(), P("tm", "row"), P("tm"), P("tm", None))
    return jax.shard_map(
        body, mesh=mesh, in_specs=placed, out_specs=P("tm", "row"), check_vma=False
    )
```
